32 devices in a mesh: patch: 2 (over x), sim: 16 (over z, y, core).
Axes of the slice: x: 2, y: 2, z: 4, core: 2. Of those that a mesh axis runs over, the one named last changes fastest.
Arguments:
- sky_maps: bfloat16 [2048, 2048], P(('patch', 'sim')), parts along dimension 0, may hold values from -6 to 6
- ivf_maps: bfloat16 [2048, 2048], P(('patch', 'sim')), parts along dimension 0, may hold values from -6 to 6
- sim_sky: bfloat16 [8, 2048, 2048], P(None, ('patch', 'sim')), parts along dimension 1, may hold values from -6 to 6
- sim_ivf: bfloat16 [8, 2048, 2048], P(None, ('patch', 'sim')), parts along dimension 1, may hold values from -6 to 6
- ra_wiener: bfloat16 [1024, 1024], replicated, may hold values from -0.1875 to 0.1875
- ra_gradient: bfloat16 [1024, 1024], replicated, may hold values from -0.1875 to 0.1875
- pair_table: int32 [8, 8], replicated, may hold values 0 or 1
- sim_index: int32 [4], replicated, may hold values from 0 to 7
- source_pixels: int32 [8192], P('patch'), parts along dimension 0, may hold values from 0 to 262143
- response: float32 [256], P('patch'), parts along dimension 0, may hold values from 0.2 to 2
Outputs:
- lens_split: float32 [2048, 2048], P(('patch', 'sim')), parts along dimension 0
The draws below stay inside these ranges and needn't reach their ends.
There are 2 independent parts, one for each index of `patch`. The reference program is written for one: setup_inputs(seed, part) draws one part's arguments, and reference() takes and returns one part's arrays. A program takes and returns all parts, laid end to end along the dimension named above; an argument that names none is the same for every part. Nothing has to cross between parts.
Inputs may be any that keep to these rules, and one draw needn't show every extreme that they name: `sim_index`: indices into the cached evolutions; entries may repeat. `source_pixels`: flat pixel indices of the patch; entries may repeat.
All inputs are finite; a program needn't handle non-finite values.
Results may differ from the reference program's by a relative error of at most 0.0035.
Values may be sent and summed in bfloat16 or wider, within the bound.
A program may use at most 128 MiB of HBM per device.

```python
import math
import jax
import jax.numpy as jnp
from jax import lax

NSPLIT = 8
ROWS_DEV = 64
COLS = 2048
FT = 1024
SIM_CACHE = 8
NUSE = 4
NSRC = 4096
NB = 2
NROWS = 128
SROWS = 1024


def set_ends(entries, stream_key, smallest, top_value):
    spot = [jax.random.randint(jax.random.fold_in(stream_key, axis), (), 0, length) for axis, length in enumerate(entries.shape)]
    widest = entries.shape.index(max(entries.shape))
    beside = spot[:widest] + [(spot[widest] + 1) % entries.shape[widest]] + spot[widest + 1:]
    return entries.at[tuple(spot)].set(smallest).at[tuple(beside)].set(top_value)


def block_levels(own_key, dims, pieces, least, high):
    level, own = 1.0, jax.random.fold_in(own_key, 6)
    for position, parts in pieces:
        draws = jnp.exp(jax.random.uniform(jax.random.fold_in(own, position), (parts,), jnp.float32, least / len(pieces), high / len(pieces)))
        level = level * jnp.repeat(draws, dims[position] // parts).reshape([-1 if axis == position else 1 for axis in range(len(dims))])
    return level


def centred(own_key, dims, scale, bound, shards=(), held_as=jnp.bfloat16):
    factor_of = block_levels(own_key, dims, shards, -0.22, 0.18) if shards else 1.0
    entries = jax.random.normal(own_key, dims, jnp.float32) * scale * factor_of
    return jnp.minimum(jnp.maximum(entries, -bound), bound).astype(held_as)


def setup_inputs(seed: int = 0, part: int = 0) -> dict:
    splits = jax.random.split(jax.random.key(seed), 11)
    own_keys = jax.random.split(jax.random.fold_in(splits[10], part), 11)
    sky_maps = centred(own_keys[0], (SROWS, COLS), 1.0, 6.0, ((0, 16),))
    ivf_maps = centred(own_keys[1], (SROWS, COLS), 1.0, 6.0, ((0, 16),))
    sim_sky = centred(own_keys[2], (SIM_CACHE, SROWS, COLS), 1.0, 6.0, ((1, 16),))
    sim_ivf = centred(own_keys[3], (SIM_CACHE, SROWS, COLS), 1.0, 6.0, ((1, 16),))
    ra_wiener = centred(splits[4], (FT, FT), FT ** -0.5, 0.1875)
    ra_gradient = centred(splits[5], (FT, FT), FT ** -0.5, 0.1875)
    pair_table = set_ends((jax.random.randint(splits[6], (NSPLIT, NSPLIT), 0, 4) < 3).astype(jnp.int32), jax.random.fold_in(splits[6], 1), 0, 1)
    sim_index = set_ends(jax.random.randint(splits[7], (NUSE,), 0, SIM_CACHE), jax.random.fold_in(splits[7], 1), 0, SIM_CACHE - 1).astype(jnp.int32)
    source_pixels = set_ends(jax.random.randint(own_keys[8], (NSRC,), 0, NROWS * COLS), jax.random.fold_in(own_keys[8], 1), 0, (NROWS * COLS) - 1).astype(jnp.int32)
    response = jnp.clip(jnp.exp(jax.random.uniform(own_keys[9], (NROWS,), jnp.float32, math.log(0.2), math.log(2.0))), 0.2, 2.0)
    return {"sky_maps": sky_maps, "ivf_maps": ivf_maps, "sim_sky": sim_sky, "sim_ivf": sim_ivf, "ra_wiener": ra_wiener, "ra_gradient": ra_gradient, "pair_table": pair_table, "sim_index": sim_index, "source_pixels": source_pixels, "response": response}


def tile_apply(values, matrix):
    width = matrix.shape[0]
    shaped = values.reshape(values.shape[:-1] + (values.shape[-1] // width, width)).astype(jnp.float32)
    result = jnp.einsum("...tc,cd->...td", shaped, matrix.astype(jnp.float32))
    return result.reshape(values.shape)


def row_slope(values):
    padded = jnp.pad(values.astype(jnp.float32), ((0, 0), (1, 1), (0, 0)))
    return (padded[:, 2:] - padded[:, :-2]) * 0.5


def estimate(sky, ivf, keep, pair_weights, ra_wiener, ra_gradient, response):
    masked = ivf * keep[None]
    wiener = tile_apply(sky, ra_wiener).astype(jnp.bfloat16)
    grad_ra = tile_apply(masked, ra_gradient)
    grad_dec = row_slope(masked)
    sum_ra = jnp.einsum("sj,jrc->src", pair_weights, grad_ra)
    sum_dec = jnp.einsum("sj,jrc->src", pair_weights, grad_dec)
    sum_src = jnp.einsum("sj,jrc->src", pair_weights, masked.astype(jnp.float32))
    wiener_wide = wiener.astype(jnp.float32)
    flux_ra = (wiener_wide * sum_ra).astype(jnp.bfloat16)
    flux_dec = wiener_wide * sum_dec
    divergence = tile_apply(flux_ra, ra_gradient) + row_slope(flux_dec)
    return -divergence - response[None, :, None] * (wiener_wide * sum_src)


def reference(sky_maps, ivf_maps, sim_sky, sim_ivf, ra_wiener, ra_gradient, pair_table, sim_index, source_pixels, response):
    offset_rows = (NB // 2) * ROWS_DEV
    hit = jnp.zeros((NROWS * COLS,), jnp.bfloat16).at[source_pixels].set(1)
    keep = (1 - hit).reshape(NROWS, COLS)
    others = 1.0 - jnp.eye(NSPLIT, dtype=jnp.float32)
    pair_weights = pair_table.astype(jnp.float32) * others
    shape3 = (NSPLIT, NROWS, COLS)

    def ordered(values):
        return jnp.roll(values, -offset_rows, axis=0).reshape(shape3)

    data_part = estimate(ordered(sky_maps), ordered(ivf_maps), keep, pair_weights, ra_wiener, ra_gradient, response)
    mean_field = jnp.zeros(shape3, jnp.float32)
    for member in range(NUSE):
        chosen = sim_index[member]
        sky_one = ordered(lax.dynamic_index_in_dim(sim_sky, chosen, 0, keepdims=False))
        ivf_one = ordered(lax.dynamic_index_in_dim(sim_ivf, chosen, 0, keepdims=False))
        mean_field = mean_field + estimate(sky_one, ivf_one, keep, pair_weights, ra_wiener, ra_gradient, response)
    result = data_part - mean_field / NUSE
    return jnp.roll(result.reshape(SROWS, COLS), offset_rows, axis=0)
```

```python
import functools

import jax
import jax.numpy as jnp
from jax import lax
from jax.experimental import pallas as pl
from jax.experimental.pallas import tpu as pltpu
from jax.sharding import PartitionSpec as P

PIECES = 2
MESH = pl.DeviceIdType.MESH


def tile_apply(values, matrix):
    width = matrix.shape[0]
    shaped = values.reshape(values.shape[:-1] + (values.shape[-1] // width, width))
    result = jnp.einsum("...tc,cd->...td", shaped, matrix, preferred_element_type=jnp.float32)
    return result.reshape(values.shape)


def pair_sums(nsplit, pair_ref, x_ref, s_ref, ro, r1, r2, ra, rb, yb, pa, pb, bb, send, recv):
    count = x_ref.shape[0]
    group = lax.axis_size("sim") // nsplit
    index = lax.axis_index("sim")
    place = index // group
    lane = index % group
    levels = nsplit // 2
    level = place // 2
    column = place % 2
    back = (lane < group // 2).astype(jnp.int32)
    low = level < levels // 2
    is_outer = (level == 0) | (level == levels - 1)

    def at(lev, col):
        return lev * 2 + col

    def device(pos):
        return {"sim": pos * group + lane}

    def weight(dest, source):
        row = (dest - back + nsplit) % nsplit
        col = (source - back + nsplit) % nsplit
        value = pair_ref[row, col].astype(jnp.float32)
        return value * (dest != source).astype(jnp.float32)

    other = 1 - column
    partner = at(level, other)
    near_outer = jnp.where(low, 0, levels - 1)
    near_inner = jnp.where(low, 1, levels - 2)
    far_inner = jnp.where(low, levels - 2, 1)
    far_outer = jnp.where(low, levels - 1, 0)

    def copy(stream, n, src, dst, pos):
        return pltpu.make_async_remote_copy(
            src_ref=src.at[n], dst_ref=dst.at[n],
            send_sem=send.at[stream, n], recv_sem=recv.at[stream, n],
            device_id=device(pos), device_id_type=MESH,
        )

    barrier = pltpu.get_barrier_semaphore()

    def greet(pos):
        pl.semaphore_signal(barrier, inc=1, device_id=device(pos), device_id_type=MESH)

    def wide(ref, n):
        return ref[n].astype(jnp.float32)

    def across(n):
        return copy(5, n, bb, yb, partner)

    def finish(n):
        across(n).wait_recv()
        s_ref[n] = s_ref[n] + wide(yb, n)

    @pl.when(is_outer)
    def _():
        inner = at(near_inner, column)
        greet(inner)
        greet(partner)
        pl.semaphore_wait(barrier, 2)

        def give(n):
            return copy(0, n, x_ref, ro, inner)

        @pl.loop(0, count)
        def _(n):
            give(n).start()

        own = weight(partner, place)

        @pl.loop(0, count)
        def _(n):
            copy(4, n, pb, rb, inner).wait_recv()
            bb[n] = (wide(rb, n) + own * wide(x_ref, n)).astype(bb.dtype)
            across(n).start()
            copy(3, n, pa, ra, inner).wait_recv()
            s_ref[n] = wide(ra, n)

        @pl.loop(0, count)
        def _(n):
            finish(n)
            give(n).wait_send()
            across(n).wait_send()

    @pl.when(jnp.logical_not(is_outer))
    def _():
        outer = at(near_outer, column)
        far = at(far_inner, column)
        edge = at(far_outer, column)
        greet(outer)
        greet(far)
        greet(partner)
        pl.semaphore_wait(barrier, 3)

        def own(n):
            return copy(1, n, x_ref, r1, far)

        def relay(n):
            return copy(2, n, ro, r2, far)

        def to_a(n):
            return copy(3, n, pa, ra, outer)

        def to_b(n):
            return copy(4, n, pb, rb, outer)

        def forward(n):
            own(n).start()
            copy(0, n, x_ref, ro, outer).wait_recv()
            relay(n).start()

        @pl.loop(0, 2)
        def _(n):
            forward(n)

        outer_other = at(near_outer, other)
        a_own, a_far, a_edge = weight(outer, place), weight(outer, far), weight(outer, edge)
        b_own, b_far, b_edge = weight(outer_other, place), weight(outer_other, far), weight(outer_other, edge)
        y_own, y_out = weight(partner, place), weight(partner, outer)
        y_far, y_edge = weight(partner, far), weight(partner, edge)
        s_out, s_far, s_edge = weight(place, outer), weight(place, far), weight(place, edge)

        @pl.loop(0, count)
        def _(n):
            @pl.when(n + 2 < count)
            def _():
                forward(n + 2)

            own(n).wait_recv()
            relay(n).wait_recv()
            mine, out, far_v, edge_v = wide(x_ref, n), wide(ro, n), wide(r1, n), wide(r2, n)
            pa[n] = (a_own * mine + a_far * far_v + a_edge * edge_v).astype(pa.dtype)
            pb[n] = (b_own * mine + b_far * far_v + b_edge * edge_v).astype(pb.dtype)
            to_b(n).start()
            to_a(n).start()
            bb[n] = (y_own * mine + y_out * out + y_far * far_v + y_edge * edge_v).astype(bb.dtype)
            across(n).start()
            s_ref[n] = s_out * out + s_far * far_v + s_edge * edge_v

        @pl.loop(0, count)
        def _(n):
            finish(n)
            own(n).wait_send()
            relay(n).wait_send()
            to_a(n).wait_send()
            to_b(n).wait_send()
            across(n).wait_send()


def gather_sums(chosen, pair_table):
    fields, rows, columns = chosen.shape
    nsplit = pair_table.shape[0]
    shape = (fields * PIECES, rows // PIECES, columns)
    buffer = pltpu.VMEM(shape, chosen.dtype)
    sums = pl.pallas_call(
        functools.partial(pair_sums, nsplit),
        out_shape=jax.ShapeDtypeStruct(shape, jnp.float32),
        in_specs=[pl.BlockSpec(memory_space=pltpu.SMEM), pl.BlockSpec(memory_space=pltpu.VMEM)],
        out_specs=pl.BlockSpec(memory_space=pltpu.VMEM),
        scratch_shapes=[buffer] * 9
        + [pltpu.SemaphoreType.DMA((6, shape[0])), pltpu.SemaphoreType.DMA((6, shape[0]))],
        compiler_params=pltpu.CompilerParams(
            collective_id=0, has_side_effects=True, vmem_limit_bytes=48 << 20
        ),
    )(pair_table, chosen.reshape(shape))
    return sums.reshape(fields, rows, columns)


def rims(cells, band_index, group_bands):
    count = lax.axis_size("sim")
    below = lax.ppermute(cells[:, -1:], "sim", [(i, (i + 1) % count) for i in range(count)])
    above = lax.ppermute(cells[:, :1], "sim", [((i + 1) % count, i) for i in range(count)])
    below = below * (band_index > 0).astype(cells.dtype)
    above = above * (band_index < group_bands - 1).astype(cells.dtype)
    return jnp.concatenate([below, cells, above], axis=1)


def row_slope(padded):
    return (padded[:, 2:] - padded[:, :-2]) * 0.5


def on_device(
    sky_maps,
    ivf_maps,
    sim_sky,
    sim_ivf,
    ra_wiener,
    ra_gradient,
    pair_table,
    sim_index,
    source_pixels,
    response,
):
    nsplit = pair_table.shape[0]
    nuse = sim_index.shape[0]
    axis_count = lax.axis_size("sim")
    group_bands = axis_count // nsplit
    logical = (lax.axis_index("sim") - group_bands // 2) % axis_count
    band_index = logical % group_bands
    rows, columns = sky_maps.shape
    chosen_sky = jnp.concatenate([sky_maps[None], jnp.take(sim_sky, sim_index, axis=0)], axis=0)
    chosen_ivf = jnp.concatenate([ivf_maps[None], jnp.take(sim_ivf, sim_index, axis=0)], axis=0)
    sums = gather_sums(chosen_ivf, pair_table)
    offsets = source_pixels - band_index * rows * columns
    inside = (offsets >= 0) & (offsets < rows * columns)
    offsets = jnp.where(inside, offsets, rows * columns)
    hit = jnp.zeros((rows * columns,), jnp.float32).at[offsets].set(1, mode="drop")
    keep = (1 - hit).reshape(rows, columns)
    sums = sums * keep[None]
    wiener = tile_apply(chosen_sky, ra_wiener).astype(jnp.bfloat16).astype(jnp.float32)
    total_ra = tile_apply(sums.astype(jnp.bfloat16), ra_gradient)
    total_dec = row_slope(rims(sums, band_index, group_bands))
    flux_ra = (wiener * total_ra).astype(jnp.bfloat16).astype(jnp.float32)
    flux_dec = wiener * total_dec
    flux_src = wiener * sums

    def combine(values):
        return values[:1] - jnp.sum(values[1:], axis=0, keepdims=True) / nuse

    divergence = tile_apply(combine(flux_ra).astype(jnp.bfloat16), ra_gradient)
    divergence = divergence + row_slope(rims(combine(flux_dec), band_index, group_bands))
    weight_rows = lax.dynamic_slice_in_dim(response, band_index * rows, rows)
    return (-divergence - weight_rows[None, :, None] * combine(flux_src))[0]


def solution(mesh):
    in_specs = (
        P(("patch", "sim"), None),
        P(("patch", "sim"), None),
        P(None, ("patch", "sim"), None),
        P(None, ("patch", "sim"), None),
        P(),
        P(),
        P(),
        P(),
        P("patch"),
        P("patch"),
    )
    out_specs = P(("patch", "sim"), None)
    return jax.shard_map(
        on_device, mesh=mesh, in_specs=in_specs, out_specs=out_specs, check_vma=False
    )
```

```python
import functools

import jax
import jax.numpy as jnp
from jax import lax
from jax.experimental import pallas as pl
from jax.experimental.pallas import tpu as pltpu
from jax.sharding import PartitionSpec as P

PIECES = 2
LANES = 128
SLAB = 8
MESH = pl.DeviceIdType.MESH


def pick(index_ref, maps_a, maps_b, sim_a, sim_b, out_a, out_b):
    @pl.when(pl.program_id(0) == 0)
    def _():
        out_a[0] = maps_a[...]
        out_b[0] = maps_b[...]

    @pl.when(pl.program_id(0) > 0)
    def _():
        out_a[...] = sim_a[...]
        out_b[...] = sim_b[...]


def choose(sim_index, maps_a, maps_b, sim_a, sim_b):
    rows, columns = maps_a.shape
    fields = sim_index.shape[0] + 1
    whole = pl.BlockSpec((rows, columns), lambda f, ids: (0, 0))
    picked = pl.BlockSpec((1, rows, columns), lambda f, ids: (ids[jnp.maximum(f - 1, 0)], 0, 0))
    placed = pl.BlockSpec((1, rows, columns), lambda f, ids: (f, 0, 0))
    shape = jax.ShapeDtypeStruct((fields, rows, columns), maps_a.dtype)
    return pl.pallas_call(
        pick,
        grid_spec=pltpu.PrefetchScalarGridSpec(
            num_scalar_prefetch=1, grid=(fields,),
            in_specs=[whole, whole, picked, picked], out_specs=[placed, placed],
        ),
        out_shape=[shape, shape],
    )(sim_index, maps_a, maps_b, sim_a, sim_b)


def estimator(
    nsplit, pair_ref, x_ref, sky_ref, wiener_ref, grad_ref, key_ref, lane_ref, resp_ref, out_ref,
    ro, r1, r2, ra, rb, yb, pa, pb, bb, sums, keep, sm, wf, acc_f, acc_d, acc_s,
    up_w, dn_w, bl_w, ab_w, up_e, dn_e, bl_e, ab_e, send, recv, slab_send, slab_recv,
):
    count = x_ref.shape[0]
    fields, rows, columns = sky_ref.shape
    part = rows // PIECES
    width = grad_ref.shape[0]
    tiles = columns // width
    f32, bf16 = jnp.float32, jnp.bfloat16
    devices = lax.axis_size("sim")
    group = devices // nsplit
    index = lax.axis_index("sim")
    place = index // group
    lane = index % group
    band = (lane - group // 2 + group) % group
    levels = nsplit // 2
    level = place // 2
    column = place % 2
    back = (lane < group // 2).astype(jnp.int32)
    low = level < levels // 2
    is_outer = (level == 0) | (level == levels - 1)
    is_inner = jnp.logical_not(is_outer)
    has_above = band < group - 1
    has_below = band > 0

    def at(lev, col):
        return lev * 2 + col

    def device(pos):
        return {"sim": pos * group + lane}

    def weight(dest, source):
        row = (dest - back + nsplit) % nsplit
        col = (source - back + nsplit) % nsplit
        value = pair_ref[row, col].astype(f32)
        return value * (dest != source).astype(f32)

    other = 1 - column
    partner = at(level, other)
    near_outer = jnp.where(low, 0, levels - 1)
    near_inner = jnp.where(low, 1, levels - 2)
    far_inner = jnp.where(low, levels - 2, 1)
    far_outer = jnp.where(low, levels - 1, 0)
    inner = at(near_inner, column)
    outer = at(near_outer, column)
    far = at(far_inner, column)
    edge = at(far_outer, column)
    above = {"sim": (index + 1) % devices}
    below = {"sim": (index + devices - 1) % devices}

    def copy(stream, n, src, dst, pos):
        return pltpu.make_async_remote_copy(
            src_ref=src.at[n], dst_ref=dst.at[n],
            send_sem=send.at[stream, n], recv_sem=recv.at[stream, n],
            device_id=device(pos), device_id_type=MESH,
        )

    def slab(which, src, dst, target):
        return pltpu.make_async_remote_copy(
            src_ref=src, dst_ref=dst,
            send_sem=slab_send.at[which], recv_sem=slab_recv.at[which],
            device_id=target, device_id_type=MESH,
        )

    wiener_up = slab(0, up_w, bl_w, above)
    wiener_down = slab(1, dn_w, ab_w, below)
    edge_up = slab(2, up_e, bl_e, above)
    edge_down = slab(3, dn_e, ab_e, below)

    def wide(ref, n):
        return ref[n].astype(f32)

    def across(n):
        return copy(5, n, bb, yb, partner)

    def give(n):
        return copy(0, n, x_ref, ro, inner)

    def own(n):
        return copy(1, n, x_ref, r1, far)

    def relay(n):
        return copy(2, n, ro, r2, far)

    def to_a(n):
        return copy(3, n, pa, ra, outer)

    def to_b(n):
        return copy(4, n, pb, rb, outer)

    def forward(n):
        own(n).start()
        copy(0, n, x_ref, ro, outer).wait_recv()
        relay(n).start()

    barrier = pltpu.get_barrier_semaphore()

    def greet(target):
        pl.semaphore_signal(barrier, inc=1, device_id=target, device_id_type=MESH)

    greet(device(partner))

    @pl.when(has_above)
    def _():
        greet(above)

    @pl.when(has_below)
    def _():
        greet(below)

    @pl.when(is_outer)
    def _():
        greet(device(inner))

    @pl.when(is_inner)
    def _():
        greet(device(outer))
        greet(device(far))

    met = 2 + is_inner.astype(jnp.int32) + has_above.astype(jnp.int32) + has_below.astype(jnp.int32)
    pl.semaphore_wait(barrier, met)

    @pl.when(is_outer)
    def _():
        @pl.loop(0, count)
        def _(n):
            give(n).start()

    @pl.when(is_inner)
    def _():
        @pl.loop(0, 2)
        def _(n):
            forward(n)

    acc_f[...] = jnp.zeros_like(acc_f)
    acc_d[...] = jnp.zeros_like(acc_d)
    acc_s[...] = jnp.zeros_like(acc_s)
    up_e[...] = jnp.zeros_like(up_e)
    dn_e[...] = jnp.zeros_like(dn_e)
    up_w[...] = jnp.zeros_like(up_w)
    dn_w[...] = jnp.zeros_like(dn_w)

    @pl.when(jnp.logical_not(has_above))
    def _():
        ab_w[...] = jnp.zeros_like(ab_w)
        ab_e[...] = jnp.zeros_like(ab_e)

    @pl.when(jnp.logical_not(has_below))
    def _():
        bl_w[...] = jnp.zeros_like(bl_w)
        bl_e[...] = jnp.zeros_like(bl_e)

    outer_other = at(near_outer, other)
    y_out_own = weight(partner, place)
    a_far, a_edge, a_own = weight(outer, far), weight(outer, edge), weight(outer, place)
    b_far, b_edge, b_own = weight(outer_other, far), weight(outer_other, edge), weight(outer_other, place)
    y_out, y_far, y_edge = weight(partner, outer), weight(partner, far), weight(partner, edge)
    s_out, s_far, s_edge = weight(place, outer), weight(place, far), weight(place, edge)

    def outer_piece(n):
        copy(4, n, pb, rb, inner).wait_recv()
        bb[n] = (wide(rb, n) + y_out_own * wide(x_ref, n)).astype(bf16)
        across(n).start()
        copy(3, n, pa, ra, inner).wait_recv()
        sums[n] = wide(ra, n)

    def inner_piece(n):
        @pl.when(n + 2 < count)
        def _():
            forward(n + 2)

        own(n).wait_recv()
        relay(n).wait_recv()
        mine, out, far_v, edge_v = wide(x_ref, n), wide(ro, n), wide(r1, n), wide(r2, n)
        pb[n] = (b_own * mine + b_far * far_v + b_edge * edge_v).astype(bf16)
        pa[n] = (a_own * mine + a_far * far_v + a_edge * edge_v).astype(bf16)
        to_b(n).start()
        to_a(n).start()
        bb[n] = (y_out_own * mine + y_out * out + y_far * far_v + y_edge * edge_v).astype(bf16)
        across(n).start()
        sums[n] = s_out * out + s_far * far_v + s_edge * edge_v

    def tile_dot(values):
        high = values.astype(bf16)
        rest = (values - high.astype(f32)).astype(bf16)
        lefts = [half[:, t * width:(t + 1) * width] for half in (high, rest) for t in range(tiles)]
        result = jnp.dot(jnp.concatenate(lefts, axis=0), grad_ref[...], preferred_element_type=f32)
        blocks = [
            result[t * rows:(t + 1) * rows] + result[(tiles + t) * rows:(tiles + t + 1) * rows]
            for t in range(tiles)
        ]
        return jnp.concatenate(blocks, axis=1)

    row_of = lax.broadcasted_iota(jnp.int32, (rows, columns), 0)

    def slope(values, before, after):
        upper = jnp.where(row_of == rows - 1, after, pltpu.roll(values, rows - 1, 0))
        lower = jnp.where(row_of == 0, before, pltpu.roll(values, 1, 0))
        return (upper - lower) * 0.5

    def share(f):
        return jnp.where(f == 0, jnp.float32(1.0), jnp.float32(-1.0 / (fields - 1)))

    def filter_sky(f):
        sky = sky_ref[f]
        lefts = [sky[:, t * width:(t + 1) * width] for t in range(tiles)]
        result = jnp.dot(jnp.concatenate(lefts, axis=0), wiener_ref[...], preferred_element_type=f32)
        result = result.astype(bf16).astype(f32)
        for t in range(tiles):
            wf[f, :, t * width:(t + 1) * width] = result[t * rows:(t + 1) * rows]
        up_w[pl.ds(f, 1), :] = wf[f, rows - 1:rows, :]
        dn_w[pl.ds(f, 1), :] = wf[f, 0:1, :]

    def mask():
        cells = rows * columns // LANES
        total = key_ref.shape[1]
        chunk = 512 if total % 512 == 0 else total
        cell_of = lax.broadcasted_iota(jnp.int32, (cells, chunk), 0)
        lane_of = lax.broadcasted_iota(jnp.int32, (LANES, chunk), 0)
        hits = jnp.zeros((cells, LANES), f32)
        for start in range(0, total, chunk):
            keys = key_ref[:, start:start + chunk]
            lanes = lane_ref[:, start:start + chunk]
            left = jnp.where(cell_of == keys, 1.0, 0.0).astype(bf16)
            right = jnp.where(lane_of == lanes, 1.0, 0.0).astype(bf16)
            hits = hits + lax.dot_general(
                left, right, (((1,), (1,)), ((), ())), preferred_element_type=f32
            )
        kept = jnp.where(hits > 0.5, 0.0, 1.0)
        for c in range(columns // LANES):
            keep[:, c * LANES:(c + 1) * LANES] = kept[c * rows:(c + 1) * rows]

    def field(f):
        for piece in range(PIECES):
            n = f * PIECES + piece
            span = slice(piece * part, (piece + 1) * part)
            across(n).wait_recv()
            sm[span, :] = (sums[n] + wide(yb, n)) * keep[span, :]
        total = sm[...]
        factor = share(f)
        flux = (wf[f] * tile_dot(total)).astype(bf16).astype(f32)
        acc_f[...] += factor * flux
        scaled = factor * wf[f]
        acc_s[...] += scaled * total
        acc_d[...] += scaled * slope(total, 0.0, 0.0)
        up_e[pl.ds(f, 1), :] = sm[rows - 1:rows, :]
        dn_e[pl.ds(f, 1), :] = sm[0:1, :]
        up_e[fields:fields + 1, :] += factor * wf[f, rows - 1:rows, :] * sm[rows - 2:rows - 1, :]
        dn_e[fields:fields + 1, :] += factor * wf[f, 0:1, :] * sm[1:2, :]

    @pl.loop(0, fields)
    def _(f):
        @pl.when(is_outer)
        def _():
            @pl.loop(0, PIECES)
            def _(piece):
                outer_piece(f * PIECES + piece)

        @pl.when(is_inner)
        def _():
            @pl.loop(0, PIECES)
            def _(piece):
                inner_piece(f * PIECES + piece)

        filter_sky(f)

        @pl.when(f == 0)
        def _():
            mask()

        @pl.when((f == fields - 1) & has_above)
        def _():
            wiener_up.start()

        @pl.when((f == fields - 1) & has_below)
        def _():
            wiener_down.start()

        @pl.when(f > 0)
        def _():
            field(f - 1)

    field(fields - 1)

    @pl.when(has_above)
    def _():
        edge_up.start()

    @pl.when(has_below)
    def _():
        edge_down.start()

    sm[...] = tile_dot(acc_f[...])

    @pl.when(has_above)
    def _():
        wiener_down.wait_recv()
        edge_down.wait_recv()

    @pl.when(has_below)
    def _():
        wiener_up.wait_recv()
        edge_up.wait_recv()

    zero = jnp.zeros((1, columns), f32)
    top, bottom = zero, zero
    after, before = ab_e[fields:fields + 1, :], -bl_e[fields:fields + 1, :]
    for f in range(fields):
        factor = 1.0 if f == 0 else -1.0 / (fields - 1)
        one = slice(f, f + 1)
        top = top + factor * wf[f, rows - 1:rows, :] * ab_e[one, :]
        bottom = bottom - factor * wf[f, 0:1, :] * bl_e[one, :]
        after = after - factor * ab_w[one, :] * up_e[one, :]
        before = before + factor * bl_w[one, :] * dn_e[one, :]
    flux_dec = acc_d[...] + jnp.where(row_of == rows - 1, top * 0.5, 0.0)
    flux_dec = flux_dec + jnp.where(row_of == 0, bottom * 0.5, 0.0)
    divergence = sm[...] + slope(flux_dec, before * 0.5, after * 0.5)
    out_ref[...] = -divergence - resp_ref[...] * acc_s[...]

    @pl.when(has_above)
    def _():
        wiener_up.wait_send()
        edge_up.wait_send()

    @pl.when(has_below)
    def _():
        wiener_down.wait_send()
        edge_down.wait_send()

    @pl.when(is_outer)
    def _():
        @pl.loop(0, count)
        def _(n):
            give(n).wait_send()
            across(n).wait_send()

    @pl.when(is_inner)
    def _():
        @pl.loop(0, count)
        def _(n):
            own(n).wait_send()
            relay(n).wait_send()
            to_a(n).wait_send()
            to_b(n).wait_send()
            across(n).wait_send()


def on_device(
    sky_maps,
    ivf_maps,
    sim_sky,
    sim_ivf,
    ra_wiener,
    ra_gradient,
    pair_table,
    sim_index,
    source_pixels,
    response,
):
    nsplit = pair_table.shape[0]
    axis_count = lax.axis_size("sim")
    group_bands = axis_count // nsplit
    logical = (lax.axis_index("sim") - group_bands // 2) % axis_count
    band_index = logical % group_bands
    rows, columns = sky_maps.shape
    fields = sim_index.shape[0] + 1
    sky, ivf = choose(sim_index, sky_maps, ivf_maps, sim_sky, sim_ivf)
    row = source_pixels // columns - band_index * rows
    place = source_pixels % columns
    inside = (row >= 0) & (row < rows)
    keys = jnp.where(inside, (place // LANES) * rows + row, -1)
    weight_rows = lax.dynamic_slice_in_dim(response, band_index * rows, rows)
    shape = (fields * PIECES, rows // PIECES, columns)
    slab_rows = -(-(fields + 1) // SLAB) * SLAB
    piece = pltpu.VMEM(shape, ivf.dtype)
    plane = pltpu.VMEM((rows, columns), jnp.float32)
    slabs = pltpu.VMEM((slab_rows, columns), jnp.float32)
    vmem = pl.BlockSpec(memory_space=pltpu.VMEM)
    return pl.pallas_call(
        functools.partial(estimator, nsplit),
        out_shape=jax.ShapeDtypeStruct((rows, columns), jnp.float32),
        in_specs=[pl.BlockSpec(memory_space=pltpu.SMEM)] + [vmem] * 7,
        out_specs=vmem,
        scratch_shapes=[piece] * 9
        + [pltpu.VMEM(shape, jnp.float32), plane, plane]
        + [pltpu.VMEM((fields, rows, columns), jnp.float32), plane, plane, plane]
        + [slabs] * 8
        + [pltpu.SemaphoreType.DMA((6, shape[0])), pltpu.SemaphoreType.DMA((6, shape[0]))]
        + [pltpu.SemaphoreType.DMA((4,)), pltpu.SemaphoreType.DMA((4,))],
        compiler_params=pltpu.CompilerParams(
            collective_id=0, has_side_effects=True, vmem_limit_bytes=56 << 20
        ),
    )(
        pair_table, ivf.reshape(shape), sky, ra_wiener, ra_gradient,
        keys[None], (place % LANES)[None], weight_rows[:, None],
    )


def solution(mesh):
    in_specs = (
        P(("patch", "sim"), None),
        P(("patch", "sim"), None),
        P(None, ("patch", "sim"), None),
        P(None, ("patch", "sim"), None),
        P(),
        P(),
        P(),
        P(),
        P("patch"),
        P("patch"),
    )
    out_specs = P(("patch", "sim"), None)
    return jax.shard_map(
        on_device, mesh=mesh, in_specs=in_specs, out_specs=out_specs, check_vma=False
    )
```

```python
import functools

import jax
import jax.numpy as jnp
from jax import lax
from jax.experimental import pallas as pl
from jax.experimental.pallas import tpu as pltpu
from jax.sharding import PartitionSpec as P

PIECES = 4
LANES = 128
SLAB = 8
MESH = pl.DeviceIdType.MESH


def pick(index_ref, maps_a, maps_b, sim_a, sim_b, out_a, out_b, sems):
    fields = out_a.shape[0]
    copies = []
    for f in range(fields):
        for side, (maps, sim, out) in enumerate(((maps_b, sim_b, out_b), (maps_a, sim_a, out_a))):
            source = maps if f == 0 else sim.at[index_ref[f - 1]]
            copies.append(pltpu.make_async_copy(source, out.at[f], sems.at[side, f]))
    for one in copies:
        one.start()
    for one in copies:
        one.wait()


def choose(sim_index, maps_a, maps_b, sim_a, sim_b):
    rows, columns = maps_a.shape
    fields = sim_index.shape[0] + 1
    away = pl.BlockSpec(memory_space=pl.ANY)
    vmem = pl.BlockSpec(memory_space=pltpu.VMEM)
    shape = jax.ShapeDtypeStruct((fields, rows, columns), maps_a.dtype)
    return pl.pallas_call(
        pick,
        in_specs=[pl.BlockSpec(memory_space=pltpu.SMEM)] + [away] * 4,
        out_specs=[vmem, vmem],
        out_shape=[shape, shape],
        scratch_shapes=[pltpu.SemaphoreType.DMA((2, fields))],
    )(sim_index, maps_a, maps_b, sim_a, sim_b)


def estimator(
    nsplit, pair_ref, x_ref, sky_ref, wiener_ref, grad_ref, key_ref, lane_ref, resp_ref, out_ref,
    ro, r1, r2, ra, rb, yb, pa, pb, bb, sums, keep, sm, wf, acc_f, acc_d, acc_s,
    up_w, dn_w, bl_w, ab_w, up_e, dn_e, bl_e, ab_e, hits, send, recv, slab_send, slab_recv,
):
    count = x_ref.shape[0]
    fields, rows, columns = sky_ref.shape
    part = rows // PIECES
    width = grad_ref.shape[0]
    tiles = columns // width
    f32, bf16 = jnp.float32, jnp.bfloat16
    devices = lax.axis_size("sim")
    group = devices // nsplit
    index = lax.axis_index("sim")
    place = index // group
    lane = index % group
    band = (lane - group // 2 + group) % group
    levels = nsplit // 2
    level = place // 2
    column = place % 2
    back = (lane < group // 2).astype(jnp.int32)
    low = level < levels // 2
    is_outer = (level == 0) | (level == levels - 1)
    is_inner = jnp.logical_not(is_outer)
    has_above = band < group - 1
    has_below = band > 0

    def at(lev, col):
        return lev * 2 + col

    def device(pos):
        return {"sim": pos * group + lane}

    def weight(dest, source):
        row = (dest - back + nsplit) % nsplit
        col = (source - back + nsplit) % nsplit
        value = pair_ref[row, col].astype(f32)
        return value * (dest != source).astype(f32)

    other = 1 - column
    partner = at(level, other)
    near_outer = jnp.where(low, 0, levels - 1)
    near_inner = jnp.where(low, 1, levels - 2)
    far_inner = jnp.where(low, levels - 2, 1)
    far_outer = jnp.where(low, levels - 1, 0)
    inner = at(near_inner, column)
    outer = at(near_outer, column)
    far = at(far_inner, column)
    edge = at(far_outer, column)
    above = {"sim": (index + 1) % devices}
    below = {"sim": (index + devices - 1) % devices}

    def copy(stream, n, src, dst, pos):
        return pltpu.make_async_remote_copy(
            src_ref=src.at[n], dst_ref=dst.at[n],
            send_sem=send.at[stream, n], recv_sem=recv.at[stream, n],
            device_id=device(pos), device_id_type=MESH,
        )

    def slab(which, src, dst, target):
        return pltpu.make_async_remote_copy(
            src_ref=src, dst_ref=dst,
            send_sem=slab_send.at[which], recv_sem=slab_recv.at[which],
            device_id=target, device_id_type=MESH,
        )

    wiener_up = slab(0, up_w, bl_w, above)
    wiener_down = slab(1, dn_w, ab_w, below)
    edge_up = slab(2, up_e, bl_e, above)
    edge_down = slab(3, dn_e, ab_e, below)

    def wide(ref, n):
        return ref[n].astype(f32)

    def across(n):
        return copy(5, n, bb, yb, partner)

    def give(n):
        return copy(0, n, x_ref, ro, inner)

    def own(n):
        return copy(1, n, x_ref, r1, far)

    def relay(n):
        return copy(2, n, ro, r2, far)

    def to_a(n):
        return copy(3, n, pa, ra, outer)

    def to_b(n):
        return copy(4, n, pb, rb, outer)

    def forward(n):
        own(n).start()
        copy(0, n, x_ref, ro, outer).wait_recv()
        relay(n).start()

    barrier = pltpu.get_barrier_semaphore()

    def greet(target):
        pl.semaphore_signal(barrier, inc=1, device_id=target, device_id_type=MESH)

    greet(device(partner))

    @pl.when(has_above)
    def _():
        greet(above)

    @pl.when(has_below)
    def _():
        greet(below)

    @pl.when(is_outer)
    def _():
        greet(device(inner))

    @pl.when(is_inner)
    def _():
        greet(device(outer))
        greet(device(far))

    met = 2 + is_inner.astype(jnp.int32) + has_above.astype(jnp.int32) + has_below.astype(jnp.int32)
    pl.semaphore_wait(barrier, met)

    @pl.when(is_outer)
    def _():
        @pl.loop(0, count)
        def _(n):
            give(n).start()

    @pl.when(is_inner)
    def _():
        @pl.loop(0, PIECES)
        def _(n):
            forward(n)

    acc_f[...] = jnp.zeros_like(acc_f)
    acc_d[...] = jnp.zeros_like(acc_d)
    acc_s[...] = jnp.zeros_like(acc_s)
    up_e[...] = jnp.zeros_like(up_e)
    dn_e[...] = jnp.zeros_like(dn_e)
    up_w[...] = jnp.zeros_like(up_w)
    dn_w[...] = jnp.zeros_like(dn_w)

    @pl.when(jnp.logical_not(has_above))
    def _():
        ab_w[...] = jnp.zeros_like(ab_w)
        ab_e[...] = jnp.zeros_like(ab_e)

    @pl.when(jnp.logical_not(has_below))
    def _():
        bl_w[...] = jnp.zeros_like(bl_w)
        bl_e[...] = jnp.zeros_like(bl_e)

    outer_other = at(near_outer, other)
    y_out_own = weight(partner, place)
    a_far, a_edge, a_own = weight(outer, far), weight(outer, edge), weight(outer, place)
    b_far, b_edge, b_own = weight(outer_other, far), weight(outer_other, edge), weight(outer_other, place)
    y_out, y_far, y_edge = weight(partner, outer), weight(partner, far), weight(partner, edge)
    s_out, s_far, s_edge = weight(place, outer), weight(place, far), weight(place, edge)

    def outer_piece(n):
        copy(4, n, pb, rb, inner).wait_recv()
        bb[n] = (wide(rb, n) + y_out_own * wide(x_ref, n)).astype(bf16)
        across(n).start()
        copy(3, n, pa, ra, inner).wait_recv()
        sums[n] = wide(ra, n)

    def inner_piece(n):
        @pl.when(n + PIECES < count)
        def _():
            forward(n + PIECES)

        own(n).wait_recv()
        relay(n).wait_recv()
        mine, out, far_v, edge_v = wide(x_ref, n), wide(ro, n), wide(r1, n), wide(r2, n)
        pb[n] = (b_own * mine + b_far * far_v + b_edge * edge_v).astype(bf16)
        pa[n] = (a_own * mine + a_far * far_v + a_edge * edge_v).astype(bf16)
        to_b(n).start()
        to_a(n).start()
        bb[n] = (y_out_own * mine + y_out * out + y_far * far_v + y_edge * edge_v).astype(bf16)
        across(n).start()
        sums[n] = s_out * out + s_far * far_v + s_edge * edge_v

    def tile_dot(values):
        high = values.astype(bf16)
        rest = (values - high.astype(f32)).astype(bf16)
        lefts = [half[:, t * width:(t + 1) * width] for half in (high, rest) for t in range(tiles)]
        result = jnp.dot(jnp.concatenate(lefts, axis=0), grad_ref[...], preferred_element_type=f32)
        blocks = [
            result[t * rows:(t + 1) * rows] + result[(tiles + t) * rows:(tiles + t + 1) * rows]
            for t in range(tiles)
        ]
        return jnp.concatenate(blocks, axis=1)

    row_of = lax.broadcasted_iota(jnp.int32, (rows, columns), 0)

    def slope(values, before, after):
        upper = jnp.where(row_of == rows - 1, after, pltpu.roll(values, rows - 1, 0))
        lower = jnp.where(row_of == 0, before, pltpu.roll(values, 1, 0))
        return (upper - lower) * 0.5

    def share(f):
        return jnp.where(f == 0, jnp.float32(1.0), jnp.float32(-1.0 / (fields - 1)))

    def filter_sky(f):
        sky = sky_ref[f]
        lefts = [sky[:, t * width:(t + 1) * width] for t in range(tiles)]
        result = jnp.dot(jnp.concatenate(lefts, axis=0), wiener_ref[...], preferred_element_type=f32)
        result = result.astype(bf16).astype(f32)
        for t in range(tiles):
            wf[f, :, t * width:(t + 1) * width] = result[t * rows:(t + 1) * rows]
        up_w[pl.ds(f, 1), :] = wf[f, rows - 1:rows, :]
        dn_w[pl.ds(f, 1), :] = wf[f, 0:1, :]

    cells = rows * columns // LANES
    sources = key_ref.shape[1] // PIECES

    def mask(piece):
        cell_of = lax.broadcasted_iota(jnp.int32, (cells, sources), 0)
        lane_of = lax.broadcasted_iota(jnp.int32, (LANES, sources), 0)
        span = slice(piece * sources, (piece + 1) * sources)
        left = jnp.where(cell_of == key_ref[:, span], 1.0, 0.0).astype(bf16)
        right = jnp.where(lane_of == lane_ref[:, span], 1.0, 0.0).astype(bf16)
        found = lax.dot_general(left, right, (((1,), (1,)), ((), ())), preferred_element_type=f32)
        hits[...] = found if piece == 0 else hits[...] + found

    def mask_done():
        for c in range(columns // LANES):
            block = hits[c * rows:(c + 1) * rows]
            keep[:, c * LANES:(c + 1) * LANES] = jnp.where(block > 0.5, 0.0, 1.0)

    def assemble(f):
        for piece in range(PIECES):
            n = f * PIECES + piece
            span = slice(piece * part, (piece + 1) * part)
            across(n).wait_recv()
            sm[span, :] = (sums[n] + wide(yb, n)) * keep[span, :]
        factor = share(f)
        up_e[pl.ds(f, 1), :] = sm[rows - 1:rows, :]
        dn_e[pl.ds(f, 1), :] = sm[0:1, :]
        up_e[fields:fields + 1, :] += factor * wf[f, rows - 1:rows, :] * sm[rows - 2:rows - 1, :]
        dn_e[fields:fields + 1, :] += factor * wf[f, 0:1, :] * sm[1:2, :]

    def plain_terms(f):
        total = sm[...]
        scaled = share(f) * wf[f]
        acc_s[...] += scaled * total
        acc_d[...] += scaled * slope(total, 0.0, 0.0)

    def tile_term(f):
        flux = (wf[f] * tile_dot(sm[...])).astype(bf16).astype(f32)
        acc_f[...] += share(f) * flux

    def between(f, piece):
        if piece == 0:
            filter_sky(f)

        @pl.when(f == 0)
        def _():
            mask(piece)
            if piece == PIECES - 1:
                mask_done()

        if piece == 0:
            @pl.when((f == fields - 1) & has_above)
            def _():
                wiener_up.start()

            @pl.when((f == fields - 1) & has_below)
            def _():
                wiener_down.start()

        @pl.when(f > 0)
        def _():
            if piece == 1:
                assemble(f - 1)
                plain_terms(f - 1)
            if piece == 2:
                tile_term(f - 1)

    @pl.loop(0, fields)
    def _(f):
        for piece in range(PIECES):
            n = f * PIECES + piece

            @pl.when(is_outer)
            def _():
                outer_piece(n)

            @pl.when(is_inner)
            def _():
                inner_piece(n)

            between(f, piece)

    assemble(fields - 1)
    plain_terms(fields - 1)

    @pl.when(has_above)
    def _():
        edge_up.start()

    @pl.when(has_below)
    def _():
        edge_down.start()

    tile_term(fields - 1)
    sm[...] = tile_dot(acc_f[...])

    @pl.when(has_above)
    def _():
        wiener_down.wait_recv()
        edge_down.wait_recv()

    @pl.when(has_below)
    def _():
        wiener_up.wait_recv()
        edge_up.wait_recv()

    zero = jnp.zeros((1, columns), f32)
    top, bottom = zero, zero
    after, before = ab_e[fields:fields + 1, :], -bl_e[fields:fields + 1, :]
    for f in range(fields):
        factor = 1.0 if f == 0 else -1.0 / (fields - 1)
        one = slice(f, f + 1)
        top = top + factor * wf[f, rows - 1:rows, :] * ab_e[one, :]
        bottom = bottom - factor * wf[f, 0:1, :] * bl_e[one, :]
        after = after - factor * ab_w[one, :] * up_e[one, :]
        before = before + factor * bl_w[one, :] * dn_e[one, :]
    flux_dec = acc_d[...] + jnp.where(row_of == rows - 1, top * 0.5, 0.0)
    flux_dec = flux_dec + jnp.where(row_of == 0, bottom * 0.5, 0.0)
    divergence = sm[...] + slope(flux_dec, before * 0.5, after * 0.5)
    out_ref[...] = -divergence - resp_ref[...] * acc_s[...]

    @pl.when(has_above)
    def _():
        wiener_up.wait_send()
        edge_up.wait_send()

    @pl.when(has_below)
    def _():
        wiener_down.wait_send()
        edge_down.wait_send()

    @pl.when(is_outer)
    def _():
        @pl.loop(0, count)
        def _(n):
            give(n).wait_send()
            across(n).wait_send()

    @pl.when(is_inner)
    def _():
        @pl.loop(0, count)
        def _(n):
            own(n).wait_send()
            relay(n).wait_send()
            to_a(n).wait_send()
            to_b(n).wait_send()
            across(n).wait_send()


def on_device(
    sky_maps,
    ivf_maps,
    sim_sky,
    sim_ivf,
    ra_wiener,
    ra_gradient,
    pair_table,
    sim_index,
    source_pixels,
    response,
):
    nsplit = pair_table.shape[0]
    axis_count = lax.axis_size("sim")
    group_bands = axis_count // nsplit
    logical = (lax.axis_index("sim") - group_bands // 2) % axis_count
    band_index = logical % group_bands
    rows, columns = sky_maps.shape
    fields = sim_index.shape[0] + 1
    sky, ivf = choose(sim_index, sky_maps, ivf_maps, sim_sky, sim_ivf)
    row = source_pixels // columns - band_index * rows
    place = source_pixels % columns
    inside = (row >= 0) & (row < rows)
    keys = jnp.where(inside, (place // LANES) * rows + row, -1)
    weight_rows = lax.dynamic_slice_in_dim(response, band_index * rows, rows)
    shape = (fields * PIECES, rows // PIECES, columns)
    slab_rows = -(-(fields + 1) // SLAB) * SLAB
    piece = pltpu.VMEM(shape, ivf.dtype)
    plane = pltpu.VMEM((rows, columns), jnp.float32)
    slabs = pltpu.VMEM((slab_rows, columns), jnp.float32)
    vmem = pl.BlockSpec(memory_space=pltpu.VMEM)
    return pl.pallas_call(
        functools.partial(estimator, nsplit),
        out_shape=jax.ShapeDtypeStruct((rows, columns), jnp.float32),
        in_specs=[pl.BlockSpec(memory_space=pltpu.SMEM)] + [vmem] * 7,
        out_specs=vmem,
        scratch_shapes=[piece] * 9
        + [pltpu.VMEM(shape, jnp.float32), plane, plane]
        + [pltpu.VMEM((fields, rows, columns), jnp.float32), plane, plane, plane]
        + [slabs] * 8
        + [pltpu.VMEM((rows * columns // LANES, LANES), jnp.float32)]
        + [pltpu.SemaphoreType.DMA((6, shape[0])), pltpu.SemaphoreType.DMA((6, shape[0]))]
        + [pltpu.SemaphoreType.DMA((4,)), pltpu.SemaphoreType.DMA((4,))],
        compiler_params=pltpu.CompilerParams(
            collective_id=0, has_side_effects=True, vmem_limit_bytes=56 << 20
        ),
    )(
        pair_table, ivf.reshape(shape), sky, ra_wiener, ra_gradient,
        keys[None], (place % LANES)[None], weight_rows[:, None],
    )


def solution(mesh):
    in_specs = (
        P(("patch", "sim"), None),
        P(("patch", "sim"), None),
        P(None, ("patch", "sim"), None),
        P(None, ("patch", "sim"), None),
        P(),
        P(),
        P(),
        P(),
        P("patch"),
        P("patch"),
    )
    out_specs = P(("patch", "sim"), None)
    return jax.shard_map(
        on_device, mesh=mesh, in_specs=in_specs, out_specs=out_specs, check_vma=False
    )
```

```python
import functools

import jax
import jax.numpy as jnp
from jax import lax
from jax.experimental import pallas as pl
from jax.experimental.pallas import tpu as pltpu
from jax.sharding import PartitionSpec as P

PIECES = 4
LANES = 128
SLAB = 8
MESH = pl.DeviceIdType.MESH


def pick(index_ref, maps_a, maps_b, sim_a, sim_b, out_a, out_b, sems):
    fields = out_a.shape[0]
    copies = []
    for f in range(fields):
        for side, (maps, sim, out) in enumerate(((maps_b, sim_b, out_b), (maps_a, sim_a, out_a))):
            source = maps if f == 0 else sim.at[index_ref[f - 1]]
            copies.append(pltpu.make_async_copy(source, out.at[f], sems.at[side, f]))
    for one in copies:
        one.start()
    for one in copies:
        one.wait()


def choose(sim_index, maps_a, maps_b, sim_a, sim_b):
    rows, columns = maps_a.shape
    fields = sim_index.shape[0] + 1
    away = pl.BlockSpec(memory_space=pl.ANY)
    vmem = pl.BlockSpec(memory_space=pltpu.VMEM)
    shape = jax.ShapeDtypeStruct((fields, rows, columns), maps_a.dtype)
    return pl.pallas_call(
        pick,
        in_specs=[pl.BlockSpec(memory_space=pltpu.SMEM)] + [away] * 4,
        out_specs=[vmem, vmem],
        out_shape=[shape, shape],
        scratch_shapes=[pltpu.SemaphoreType.DMA((2, fields))],
    )(sim_index, maps_a, maps_b, sim_a, sim_b)


def estimator(
    nsplit, pair_ref, x_ref, sky_far, wiener_far, grad_far, pixel_ref, resp_ref, out_ref,
    sky_ref, wiener_ref, grad_ref, key_ref, lane_ref, fetch,
    ro, r1, r2, ra, rb, yb, pa, pb, bb, sums, keep, sm, wf, acc_f, acc_d, acc_s,
    up_w, dn_w, bl_w, ab_w, up_e, dn_e, bl_e, ab_e, hits, send, recv, slab_send, slab_recv,
):
    count = x_ref.shape[0]
    fields, rows, columns = sky_ref.shape
    part = rows // PIECES
    width = grad_ref.shape[0]
    tiles = columns // width
    f32, bf16 = jnp.float32, jnp.bfloat16
    devices = lax.axis_size("sim")
    group = devices // nsplit
    index = lax.axis_index("sim")
    place = index // group
    lane = index % group
    band = (lane - group // 2 + group) % group
    levels = nsplit // 2
    level = place // 2
    column = place % 2
    back = (lane < group // 2).astype(jnp.int32)
    low = level < levels // 2
    is_outer = (level == 0) | (level == levels - 1)
    is_inner = jnp.logical_not(is_outer)
    has_above = band < group - 1
    has_below = band > 0

    def at(lev, col):
        return lev * 2 + col

    def device(pos):
        return {"sim": pos * group + lane}

    def weight(dest, source):
        row = (dest - back + nsplit) % nsplit
        col = (source - back + nsplit) % nsplit
        value = pair_ref[row, col].astype(f32)
        return value * (dest != source).astype(f32)

    other = 1 - column
    partner = at(level, other)
    near_outer = jnp.where(low, 0, levels - 1)
    near_inner = jnp.where(low, 1, levels - 2)
    far_inner = jnp.where(low, levels - 2, 1)
    far_outer = jnp.where(low, levels - 1, 0)
    inner = at(near_inner, column)
    outer = at(near_outer, column)
    far = at(far_inner, column)
    edge = at(far_outer, column)
    above = {"sim": (index + 1) % devices}
    below = {"sim": (index + devices - 1) % devices}

    def copy(stream, n, src, dst, pos):
        return pltpu.make_async_remote_copy(
            src_ref=src.at[n], dst_ref=dst.at[n],
            send_sem=send.at[stream, n], recv_sem=recv.at[stream, n],
            device_id=device(pos), device_id_type=MESH,
        )

    def slab(which, src, dst, target):
        return pltpu.make_async_remote_copy(
            src_ref=src, dst_ref=dst,
            send_sem=slab_send.at[which], recv_sem=slab_recv.at[which],
            device_id=target, device_id_type=MESH,
        )

    wiener_up = slab(0, up_w, bl_w, above)
    wiener_down = slab(1, dn_w, ab_w, below)
    edge_up = slab(2, up_e, bl_e, above)
    edge_down = slab(3, dn_e, ab_e, below)

    def wide(ref, n):
        return ref[n].astype(f32)

    def across(n):
        return copy(5, n, bb, yb, partner)

    def give(n):
        return copy(0, n, x_ref, ro, inner)

    def own(n):
        return copy(1, n, x_ref, r1, far)

    def relay(n):
        return copy(2, n, ro, r2, far)

    def to_a(n):
        return copy(3, n, pa, ra, outer)

    def to_b(n):
        return copy(4, n, pb, rb, outer)

    def forward(n):
        own(n).start()
        copy(0, n, x_ref, ro, outer).wait_recv()
        relay(n).start()

    fetches = [
        pltpu.make_async_copy(wiener_far, wiener_ref, fetch.at[0]),
        pltpu.make_async_copy(sky_far, sky_ref, fetch.at[1]),
        pltpu.make_async_copy(grad_far, grad_ref, fetch.at[2]),
    ]

    barrier = pltpu.get_barrier_semaphore()

    def greet(target):
        pl.semaphore_signal(barrier, inc=1, device_id=target, device_id_type=MESH)

    greet(device(partner))

    @pl.when(has_above)
    def _():
        greet(above)

    @pl.when(has_below)
    def _():
        greet(below)

    @pl.when(is_outer)
    def _():
        greet(device(inner))

    @pl.when(is_inner)
    def _():
        greet(device(outer))
        greet(device(far))

    met = 2 + is_inner.astype(jnp.int32) + has_above.astype(jnp.int32) + has_below.astype(jnp.int32)
    pl.semaphore_wait(barrier, met)

    @pl.when(is_outer)
    def _():
        @pl.loop(0, count)
        def _(n):
            give(n).start()

    @pl.when(is_inner)
    def _():
        @pl.loop(0, PIECES)
        def _(n):
            forward(n)

    for one in fetches:
        one.start()

    pixel = pixel_ref[...]
    pixel_row = (pixel >> (columns.bit_length() - 1)) - band * rows
    pixel_column = pixel & (columns - 1)
    block = pixel_column >> (LANES.bit_length() - 1)
    inside = (pixel_row >= 0) & (pixel_row < rows)
    key_ref[...] = jnp.where(inside, block * rows + pixel_row, -1)
    lane_ref[...] = pixel_column & (LANES - 1)
    acc_f[...] = jnp.zeros_like(acc_f)
    acc_d[...] = jnp.zeros_like(acc_d)
    acc_s[...] = jnp.zeros_like(acc_s)
    up_e[...] = jnp.zeros_like(up_e)
    dn_e[...] = jnp.zeros_like(dn_e)
    up_w[...] = jnp.zeros_like(up_w)
    dn_w[...] = jnp.zeros_like(dn_w)

    @pl.when(jnp.logical_not(has_above))
    def _():
        ab_w[...] = jnp.zeros_like(ab_w)
        ab_e[...] = jnp.zeros_like(ab_e)

    @pl.when(jnp.logical_not(has_below))
    def _():
        bl_w[...] = jnp.zeros_like(bl_w)
        bl_e[...] = jnp.zeros_like(bl_e)

    outer_other = at(near_outer, other)
    y_out_own = weight(partner, place)
    a_far, a_edge, a_own = weight(outer, far), weight(outer, edge), weight(outer, place)
    b_far, b_edge, b_own = weight(outer_other, far), weight(outer_other, edge), weight(outer_other, place)
    y_out, y_far, y_edge = weight(partner, outer), weight(partner, far), weight(partner, edge)
    s_out, s_far, s_edge = weight(place, outer), weight(place, far), weight(place, edge)

    def outer_piece(n):
        copy(4, n, pb, rb, inner).wait_recv()
        bb[n] = (wide(rb, n) + y_out_own * wide(x_ref, n)).astype(bf16)
        across(n).start()
        copy(3, n, pa, ra, inner).wait_recv()
        sums[n] = wide(ra, n)

    def inner_piece(n):
        @pl.when(n + PIECES < count)
        def _():
            forward(n + PIECES)

        own(n).wait_recv()
        relay(n).wait_recv()
        mine, out, far_v, edge_v = wide(x_ref, n), wide(ro, n), wide(r1, n), wide(r2, n)
        pb[n] = (b_own * mine + b_far * far_v + b_edge * edge_v).astype(bf16)
        pa[n] = (a_own * mine + a_far * far_v + a_edge * edge_v).astype(bf16)
        to_b(n).start()
        to_a(n).start()
        bb[n] = (y_out_own * mine + y_out * out + y_far * far_v + y_edge * edge_v).astype(bf16)
        across(n).start()
        sums[n] = s_out * out + s_far * far_v + s_edge * edge_v

    def tile_dot(values):
        high = values.astype(bf16)
        rest = (values - high.astype(f32)).astype(bf16)
        lefts = [half[:, t * width:(t + 1) * width] for half in (high, rest) for t in range(tiles)]
        result = jnp.dot(jnp.concatenate(lefts, axis=0), grad_ref[...], preferred_element_type=f32)
        blocks = [
            result[t * rows:(t + 1) * rows] + result[(tiles + t) * rows:(tiles + t + 1) * rows]
            for t in range(tiles)
        ]
        return jnp.concatenate(blocks, axis=1)

    row_of = lax.broadcasted_iota(jnp.int32, (rows, columns), 0)

    def slope(values, before, after):
        upper = jnp.where(row_of == rows - 1, after, pltpu.roll(values, rows - 1, 0))
        lower = jnp.where(row_of == 0, before, pltpu.roll(values, 1, 0))
        return (upper - lower) * 0.5

    def share(f):
        return jnp.where(f == 0, jnp.float32(1.0), jnp.float32(-1.0 / (fields - 1)))

    def filter_sky(f):
        sky = sky_ref[f]
        lefts = [sky[:, t * width:(t + 1) * width] for t in range(tiles)]
        result = jnp.dot(jnp.concatenate(lefts, axis=0), wiener_ref[...], preferred_element_type=f32)
        result = result.astype(bf16).astype(f32)
        for t in range(tiles):
            wf[f, :, t * width:(t + 1) * width] = result[t * rows:(t + 1) * rows]
        up_w[pl.ds(f, 1), :] = wf[f, rows - 1:rows, :]
        dn_w[pl.ds(f, 1), :] = wf[f, 0:1, :]

    cells = rows * columns // LANES
    sources = key_ref.shape[1] // PIECES

    def mask(piece):
        cell_of = lax.broadcasted_iota(jnp.int32, (cells, sources), 0)
        lane_of = lax.broadcasted_iota(jnp.int32, (LANES, sources), 0)
        span = slice(piece * sources, (piece + 1) * sources)
        left = jnp.where(cell_of == key_ref[:, span], 1.0, 0.0).astype(bf16)
        right = jnp.where(lane_of == lane_ref[:, span], 1.0, 0.0).astype(bf16)
        found = lax.dot_general(left, right, (((1,), (1,)), ((), ())), preferred_element_type=f32)
        hits[...] = found if piece == 0 else hits[...] + found

    def mask_done():
        for c in range(columns // LANES):
            block = hits[c * rows:(c + 1) * rows]
            keep[:, c * LANES:(c + 1) * LANES] = jnp.where(block > 0.5, 0.0, 1.0)

    def assemble(f):
        for piece in range(PIECES):
            n = f * PIECES + piece
            span = slice(piece * part, (piece + 1) * part)
            across(n).wait_recv()
            sm[span, :] = (sums[n] + wide(yb, n)) * keep[span, :]
        factor = share(f)
        up_e[pl.ds(f, 1), :] = sm[rows - 1:rows, :]
        dn_e[pl.ds(f, 1), :] = sm[0:1, :]
        up_e[fields:fields + 1, :] += factor * wf[f, rows - 1:rows, :] * sm[rows - 2:rows - 1, :]
        dn_e[fields:fields + 1, :] += factor * wf[f, 0:1, :] * sm[1:2, :]

    def plain_terms(f):
        total = sm[...]
        scaled = share(f) * wf[f]
        acc_s[...] += scaled * total
        acc_d[...] += scaled * slope(total, 0.0, 0.0)

    def tile_term(f):
        flux = (wf[f] * tile_dot(sm[...])).astype(bf16).astype(f32)
        acc_f[...] += share(f) * flux

    def between(f, piece):
        if piece == 0:
            filter_sky(f)

        @pl.when(f == 0)
        def _():
            mask(piece)
            if piece == PIECES - 1:
                mask_done()

        if piece == 0:
            @pl.when((f == fields - 1) & has_above)
            def _():
                wiener_up.start()

            @pl.when((f == fields - 1) & has_below)
            def _():
                wiener_down.start()

        @pl.when(f > 0)
        def _():
            if piece == 1:
                assemble(f - 1)
                plain_terms(f - 1)
            if piece == 2:
                tile_term(f - 1)

    for one in fetches:
        one.wait()

    @pl.loop(0, fields)
    def _(f):
        for piece in range(PIECES):
            n = f * PIECES + piece

            @pl.when(is_outer)
            def _():
                outer_piece(n)

            @pl.when(is_inner)
            def _():
                inner_piece(n)

            between(f, piece)

    assemble(fields - 1)
    plain_terms(fields - 1)

    @pl.when(has_above)
    def _():
        edge_up.start()

    @pl.when(has_below)
    def _():
        edge_down.start()

    tile_term(fields - 1)
    sm[...] = tile_dot(acc_f[...])

    @pl.when(has_above)
    def _():
        wiener_down.wait_recv()
        edge_down.wait_recv()

    @pl.when(has_below)
    def _():
        wiener_up.wait_recv()
        edge_up.wait_recv()

    zero = jnp.zeros((1, columns), f32)
    top, bottom = zero, zero
    after, before = ab_e[fields:fields + 1, :], -bl_e[fields:fields + 1, :]
    for f in range(fields):
        factor = 1.0 if f == 0 else -1.0 / (fields - 1)
        one = slice(f, f + 1)
        top = top + factor * wf[f, rows - 1:rows, :] * ab_e[one, :]
        bottom = bottom - factor * wf[f, 0:1, :] * bl_e[one, :]
        after = after - factor * ab_w[one, :] * up_e[one, :]
        before = before + factor * bl_w[one, :] * dn_e[one, :]
    flux_dec = acc_d[...] + jnp.where(row_of == rows - 1, top * 0.5, 0.0)
    flux_dec = flux_dec + jnp.where(row_of == 0, bottom * 0.5, 0.0)
    divergence = sm[...] + slope(flux_dec, before * 0.5, after * 0.5)
    span = resp_ref.shape[1]
    row_at = lax.broadcasted_iota(jnp.int32, (rows, span), 0) + band * rows
    lane_at = lax.broadcasted_iota(jnp.int32, (rows, span), 1)
    ratios = jnp.sum(jnp.where(row_at == lane_at, resp_ref[...], 0.0), axis=1, keepdims=True)
    out_ref[...] = -divergence - ratios * acc_s[...]

    @pl.when(has_above)
    def _():
        wiener_up.wait_send()
        edge_up.wait_send()

    @pl.when(has_below)
    def _():
        wiener_down.wait_send()
        edge_down.wait_send()

    @pl.when(is_outer)
    def _():
        @pl.loop(0, count)
        def _(n):
            give(n).wait_send()
            across(n).wait_send()

    @pl.when(is_inner)
    def _():
        @pl.loop(0, count)
        def _(n):
            own(n).wait_send()
            relay(n).wait_send()
            to_a(n).wait_send()
            to_b(n).wait_send()
            across(n).wait_send()


def on_device(
    sky_maps,
    ivf_maps,
    sim_sky,
    sim_ivf,
    ra_wiener,
    ra_gradient,
    pair_table,
    sim_index,
    source_pixels,
    response,
):
    nsplit = pair_table.shape[0]
    rows, columns = sky_maps.shape
    fields = sim_index.shape[0] + 1
    assert columns & (columns - 1) == 0
    sky, ivf = choose(sim_index, sky_maps, ivf_maps, sim_sky, sim_ivf)
    shape = (fields * PIECES, rows // PIECES, columns)
    slab_rows = -(-(fields + 1) // SLAB) * SLAB
    piece = pltpu.VMEM(shape, ivf.dtype)
    plane = pltpu.VMEM((rows, columns), jnp.float32)
    slabs = pltpu.VMEM((slab_rows, columns), jnp.float32)
    vmem = pl.BlockSpec(memory_space=pltpu.VMEM)
    away = pl.BlockSpec(memory_space=pl.ANY)
    pixels = pltpu.VMEM((1, source_pixels.shape[0]), jnp.int32)
    matrix = pltpu.VMEM(ra_wiener.shape, ra_wiener.dtype)
    return pl.pallas_call(
        functools.partial(estimator, nsplit),
        out_shape=jax.ShapeDtypeStruct((rows, columns), jnp.float32),
        in_specs=[pl.BlockSpec(memory_space=pltpu.SMEM), vmem] + [away] * 3 + [vmem] * 2,
        out_specs=vmem,
        scratch_shapes=[pltpu.VMEM(sky.shape, sky.dtype), matrix, matrix, pixels, pixels]
        + [pltpu.SemaphoreType.DMA((3,))] + [piece] * 9
        + [pltpu.VMEM(shape, jnp.float32), plane, plane]
        + [pltpu.VMEM((fields, rows, columns), jnp.float32), plane, plane, plane]
        + [slabs] * 8
        + [pltpu.VMEM((rows * columns // LANES, LANES), jnp.float32)]
        + [pltpu.SemaphoreType.DMA((6, shape[0])), pltpu.SemaphoreType.DMA((6, shape[0]))]
        + [pltpu.SemaphoreType.DMA((4,)), pltpu.SemaphoreType.DMA((4,))],
        compiler_params=pltpu.CompilerParams(
            collective_id=0, has_side_effects=True, vmem_limit_bytes=56 << 20
        ),
    )(
        pair_table, ivf.reshape(shape), sky, ra_wiener, ra_gradient,
        source_pixels[None], response[None],
    )


def solution(mesh):
    in_specs = (
        P(("patch", "sim"), None),
        P(("patch", "sim"), None),
        P(None, ("patch", "sim"), None),
        P(None, ("patch", "sim"), None),
        P(),
        P(),
        P(),
        P(),
        P("patch"),
        P("patch"),
    )
    out_specs = P(("patch", "sim"), None)
    return jax.shard_map(
        on_device, mesh=mesh, in_specs=in_specs, out_specs=out_specs, check_vma=False
    )
```

```python
import functools

import jax
import jax.numpy as jnp
from jax import lax
from jax.experimental import pallas as pl
from jax.experimental.pallas import tpu as pltpu
from jax.sharding import PartitionSpec as P

PIECES = 4
LANES = 128
SLAB = 8
MESH = pl.DeviceIdType.MESH


def pick(index_ref, maps, sim, out, sems):
    copies = []
    for f in range(out.shape[0]):
        source = maps if f == 0 else sim.at[index_ref[f - 1]]
        copies.append(pltpu.make_async_copy(source, out.at[f], sems.at[f]))
    for one in copies:
        one.start()
    for one in copies:
        one.wait()


def choose(sim_index, maps, sim):
    fields = sim_index.shape[0] + 1
    away = pl.BlockSpec(memory_space=pl.ANY)
    return pl.pallas_call(
        pick,
        in_specs=[pl.BlockSpec(memory_space=pltpu.SMEM), away, away],
        out_specs=pl.BlockSpec(memory_space=pltpu.VMEM),
        out_shape=jax.ShapeDtypeStruct((fields,) + maps.shape, maps.dtype),
        scratch_shapes=[pltpu.SemaphoreType.DMA((fields,))],
    )(sim_index, maps, sim)


def estimator(
    nsplit, pair_ref, index_ref, x_ref, maps_far, sim_far, wiener_far, grad_far, pixel_ref, resp_ref, out_ref,
    sky_ref, wiener_ref, grad_ref, key_ref, lane_ref, fetch,
    ro, r1, r2, ra, rb, yb, pa, pb, bb, sums, keep, sm, wf, acc_f, acc_d, acc_s,
    up_w, dn_w, bl_w, ab_w, up_e, dn_e, bl_e, ab_e, hits, send, recv, slab_send, slab_recv,
):
    count = x_ref.shape[0]
    fields = index_ref.shape[0] + 1
    rows, columns = maps_far.shape
    part = rows // PIECES
    width = grad_ref.shape[0]
    tiles = columns // width
    f32, bf16 = jnp.float32, jnp.bfloat16
    devices = lax.axis_size("sim")
    group = devices // nsplit
    index = lax.axis_index("sim")
    place = index // group
    lane = index % group
    band = (lane - group // 2 + group) % group
    levels = nsplit // 2
    level = place // 2
    column = place % 2
    back = (lane < group // 2).astype(jnp.int32)
    low = level < levels // 2
    is_outer = (level == 0) | (level == levels - 1)
    is_inner = jnp.logical_not(is_outer)
    has_above = band < group - 1
    has_below = band > 0

    def at(lev, col):
        return lev * 2 + col

    def device(pos):
        return {"sim": pos * group + lane}

    def weight(dest, source):
        row = (dest - back + nsplit) % nsplit
        col = (source - back + nsplit) % nsplit
        value = pair_ref[row, col].astype(f32)
        return value * (dest != source).astype(f32)

    other = 1 - column
    partner = at(level, other)
    near_outer = jnp.where(low, 0, levels - 1)
    near_inner = jnp.where(low, 1, levels - 2)
    far_inner = jnp.where(low, levels - 2, 1)
    far_outer = jnp.where(low, levels - 1, 0)
    inner = at(near_inner, column)
    outer = at(near_outer, column)
    far = at(far_inner, column)
    edge = at(far_outer, column)
    above = {"sim": (index + 1) % devices}
    below = {"sim": (index + devices - 1) % devices}

    def copy(stream, n, src, dst, pos):
        return pltpu.make_async_remote_copy(
            src_ref=src.at[n], dst_ref=dst.at[n],
            send_sem=send.at[stream, n], recv_sem=recv.at[stream, n],
            device_id=device(pos), device_id_type=MESH,
        )

    def slab(which, src, dst, target):
        return pltpu.make_async_remote_copy(
            src_ref=src, dst_ref=dst,
            send_sem=slab_send.at[which], recv_sem=slab_recv.at[which],
            device_id=target, device_id_type=MESH,
        )

    wiener_up = slab(0, up_w, bl_w, above)
    wiener_down = slab(1, dn_w, ab_w, below)
    edge_up = slab(2, up_e, bl_e, above)
    edge_down = slab(3, dn_e, ab_e, below)

    def wide(ref, n):
        return ref[n].astype(f32)

    def across(n):
        return copy(5, n, bb, yb, partner)

    def give(n):
        return copy(0, n, x_ref, ro, inner)

    def own(n):
        return copy(1, n, x_ref, r1, far)

    def relay(n):
        return copy(2, n, ro, r2, far)

    def to_a(n):
        return copy(3, n, pa, ra, outer)

    def to_b(n):
        return copy(4, n, pb, rb, outer)

    def forward(n):
        own(n).start()
        copy(0, n, x_ref, ro, outer).wait_recv()
        relay(n).start()

    fetches = [
        pltpu.make_async_copy(wiener_far, wiener_ref, fetch.at[0]),
        pltpu.make_async_copy(maps_far, sky_ref.at[0], fetch.at[1]),
        pltpu.make_async_copy(sim_far, sky_ref.at[pl.ds(1, sim_far.shape[0])], fetch.at[3]),
        pltpu.make_async_copy(grad_far, grad_ref, fetch.at[2]),
    ]

    barrier = pltpu.get_barrier_semaphore()

    def greet(target):
        pl.semaphore_signal(barrier, inc=1, device_id=target, device_id_type=MESH)

    greet(device(partner))

    @pl.when(has_above)
    def _():
        greet(above)

    @pl.when(has_below)
    def _():
        greet(below)

    @pl.when(is_outer)
    def _():
        greet(device(inner))

    @pl.when(is_inner)
    def _():
        greet(device(outer))
        greet(device(far))

    met = 2 + is_inner.astype(jnp.int32) + has_above.astype(jnp.int32) + has_below.astype(jnp.int32)
    pl.semaphore_wait(barrier, met)

    @pl.when(is_outer)
    def _():
        @pl.loop(0, count)
        def _(n):
            give(n).start()

    @pl.when(is_inner)
    def _():
        @pl.loop(0, PIECES)
        def _(n):
            forward(n)

    for one in fetches:
        one.start()

    pixel = pixel_ref[...]
    pixel_row = (pixel >> (columns.bit_length() - 1)) - band * rows
    pixel_column = pixel & (columns - 1)
    block = pixel_column >> (LANES.bit_length() - 1)
    inside = (pixel_row >= 0) & (pixel_row < rows)
    key_ref[...] = jnp.where(inside, block * rows + pixel_row, -1)
    lane_ref[...] = pixel_column & (LANES - 1)
    acc_f[...] = jnp.zeros_like(acc_f)
    acc_d[...] = jnp.zeros_like(acc_d)
    acc_s[...] = jnp.zeros_like(acc_s)
    up_e[...] = jnp.zeros_like(up_e)
    dn_e[...] = jnp.zeros_like(dn_e)
    up_w[...] = jnp.zeros_like(up_w)
    dn_w[...] = jnp.zeros_like(dn_w)

    @pl.when(jnp.logical_not(has_above))
    def _():
        ab_w[...] = jnp.zeros_like(ab_w)
        ab_e[...] = jnp.zeros_like(ab_e)

    @pl.when(jnp.logical_not(has_below))
    def _():
        bl_w[...] = jnp.zeros_like(bl_w)
        bl_e[...] = jnp.zeros_like(bl_e)

    outer_other = at(near_outer, other)
    y_out_own = weight(partner, place)
    a_far, a_edge, a_own = weight(outer, far), weight(outer, edge), weight(outer, place)
    b_far, b_edge, b_own = weight(outer_other, far), weight(outer_other, edge), weight(outer_other, place)
    y_out, y_far, y_edge = weight(partner, outer), weight(partner, far), weight(partner, edge)
    s_out, s_far, s_edge = weight(place, outer), weight(place, far), weight(place, edge)

    def outer_piece(n):
        copy(4, n, pb, rb, inner).wait_recv()
        bb[n] = (wide(rb, n) + y_out_own * wide(x_ref, n)).astype(bf16)
        across(n).start()
        copy(3, n, pa, ra, inner).wait_recv()
        sums[n] = wide(ra, n)

    def inner_piece(n):
        @pl.when(n + PIECES < count)
        def _():
            forward(n + PIECES)

        own(n).wait_recv()
        relay(n).wait_recv()
        mine, out, far_v, edge_v = wide(x_ref, n), wide(ro, n), wide(r1, n), wide(r2, n)
        pb[n] = (b_own * mine + b_far * far_v + b_edge * edge_v).astype(bf16)
        pa[n] = (a_own * mine + a_far * far_v + a_edge * edge_v).astype(bf16)
        to_b(n).start()
        to_a(n).start()
        bb[n] = (y_out_own * mine + y_out * out + y_far * far_v + y_edge * edge_v).astype(bf16)
        across(n).start()
        sums[n] = s_out * out + s_far * far_v + s_edge * edge_v

    def tile_dot(values):
        high = values.astype(bf16)
        rest = (values - high.astype(f32)).astype(bf16)
        lefts = [half[:, t * width:(t + 1) * width] for half in (high, rest) for t in range(tiles)]
        result = jnp.dot(jnp.concatenate(lefts, axis=0), grad_ref[...], preferred_element_type=f32)
        blocks = [
            result[t * rows:(t + 1) * rows] + result[(tiles + t) * rows:(tiles + t + 1) * rows]
            for t in range(tiles)
        ]
        return jnp.concatenate(blocks, axis=1)

    row_of = lax.broadcasted_iota(jnp.int32, (rows, columns), 0)

    def slope(values, before, after):
        upper = jnp.where(row_of == rows - 1, after, pltpu.roll(values, rows - 1, 0))
        lower = jnp.where(row_of == 0, before, pltpu.roll(values, 1, 0))
        return (upper - lower) * 0.5

    def share(f):
        return jnp.where(f == 0, jnp.float32(1.0), jnp.float32(-1.0 / (fields - 1)))

    def filter_sky(f):
        cached = index_ref[jnp.maximum(f - 1, 0)] + 1
        sky = sky_ref[jnp.where(f == 0, 0, cached)]
        lefts = [sky[:, t * width:(t + 1) * width] for t in range(tiles)]
        result = jnp.dot(jnp.concatenate(lefts, axis=0), wiener_ref[...], preferred_element_type=f32)
        result = result.astype(bf16).astype(f32)
        for t in range(tiles):
            wf[f, :, t * width:(t + 1) * width] = result[t * rows:(t + 1) * rows]
        up_w[pl.ds(f, 1), :] = wf[f, rows - 1:rows, :]
        dn_w[pl.ds(f, 1), :] = wf[f, 0:1, :]

    cells = rows * columns // LANES
    sources = key_ref.shape[1] // PIECES

    def mask(piece):
        cell_of = lax.broadcasted_iota(jnp.int32, (cells, sources), 0)
        lane_of = lax.broadcasted_iota(jnp.int32, (LANES, sources), 0)
        span = slice(piece * sources, (piece + 1) * sources)
        left = jnp.where(cell_of == key_ref[:, span], 1.0, 0.0).astype(bf16)
        right = jnp.where(lane_of == lane_ref[:, span], 1.0, 0.0).astype(bf16)
        found = lax.dot_general(left, right, (((1,), (1,)), ((), ())), preferred_element_type=f32)
        hits[...] = found if piece == 0 else hits[...] + found

    def mask_done():
        for c in range(columns // LANES):
            block = hits[c * rows:(c + 1) * rows]
            keep[:, c * LANES:(c + 1) * LANES] = jnp.where(block > 0.5, 0.0, 1.0)

    def assemble(f):
        for piece in range(PIECES):
            n = f * PIECES + piece
            span = slice(piece * part, (piece + 1) * part)
            across(n).wait_recv()
            sm[span, :] = (sums[n] + wide(yb, n)) * keep[span, :]
        factor = share(f)
        up_e[pl.ds(f, 1), :] = sm[rows - 1:rows, :]
        dn_e[pl.ds(f, 1), :] = sm[0:1, :]
        up_e[fields:fields + 1, :] += factor * wf[f, rows - 1:rows, :] * sm[rows - 2:rows - 1, :]
        dn_e[fields:fields + 1, :] += factor * wf[f, 0:1, :] * sm[1:2, :]

    def plain_terms(f):
        total = sm[...]
        scaled = share(f) * wf[f]
        acc_s[...] += scaled * total
        acc_d[...] += scaled * slope(total, 0.0, 0.0)

    def tile_term(f):
        flux = (wf[f] * tile_dot(sm[...])).astype(bf16).astype(f32)
        acc_f[...] += share(f) * flux

    def between(f, piece):
        if piece == 0:
            filter_sky(f)

        @pl.when(f == 0)
        def _():
            mask(piece)
            if piece == PIECES - 1:
                mask_done()

        if piece == 0:
            @pl.when((f == fields - 1) & has_above)
            def _():
                wiener_up.start()

            @pl.when((f == fields - 1) & has_below)
            def _():
                wiener_down.start()

        @pl.when(f > 0)
        def _():
            if piece == 1:
                assemble(f - 1)
                plain_terms(f - 1)
            if piece == 2:
                tile_term(f - 1)

    for one in fetches:
        one.wait()

    @pl.loop(0, fields)
    def _(f):
        for piece in range(PIECES):
            n = f * PIECES + piece

            @pl.when(is_outer)
            def _():
                outer_piece(n)

            @pl.when(is_inner)
            def _():
                inner_piece(n)

            between(f, piece)

    assemble(fields - 1)
    plain_terms(fields - 1)

    @pl.when(has_above)
    def _():
        edge_up.start()

    @pl.when(has_below)
    def _():
        edge_down.start()

    tile_term(fields - 1)
    sm[...] = tile_dot(acc_f[...])

    @pl.when(has_above)
    def _():
        wiener_down.wait_recv()
        edge_down.wait_recv()

    @pl.when(has_below)
    def _():
        wiener_up.wait_recv()
        edge_up.wait_recv()

    zero = jnp.zeros((1, columns), f32)
    top, bottom = zero, zero
    after, before = ab_e[fields:fields + 1, :], -bl_e[fields:fields + 1, :]
    for f in range(fields):
        factor = 1.0 if f == 0 else -1.0 / (fields - 1)
        one = slice(f, f + 1)
        top = top + factor * wf[f, rows - 1:rows, :] * ab_e[one, :]
        bottom = bottom - factor * wf[f, 0:1, :] * bl_e[one, :]
        after = after - factor * ab_w[one, :] * up_e[one, :]
        before = before + factor * bl_w[one, :] * dn_e[one, :]
    flux_dec = acc_d[...] + jnp.where(row_of == rows - 1, top * 0.5, 0.0)
    flux_dec = flux_dec + jnp.where(row_of == 0, bottom * 0.5, 0.0)
    divergence = sm[...] + slope(flux_dec, before * 0.5, after * 0.5)
    span = resp_ref.shape[1]
    row_at = lax.broadcasted_iota(jnp.int32, (rows, span), 0) + band * rows
    lane_at = lax.broadcasted_iota(jnp.int32, (rows, span), 1)
    ratios = jnp.sum(jnp.where(row_at == lane_at, resp_ref[...], 0.0), axis=1, keepdims=True)
    out_ref[...] = -divergence - ratios * acc_s[...]

    @pl.when(has_above)
    def _():
        wiener_up.wait_send()
        edge_up.wait_send()

    @pl.when(has_below)
    def _():
        wiener_down.wait_send()
        edge_down.wait_send()

    @pl.when(is_outer)
    def _():
        @pl.loop(0, count)
        def _(n):
            give(n).wait_send()
            across(n).wait_send()

    @pl.when(is_inner)
    def _():
        @pl.loop(0, count)
        def _(n):
            own(n).wait_send()
            relay(n).wait_send()
            to_a(n).wait_send()
            to_b(n).wait_send()
            across(n).wait_send()


def on_device(
    sky_maps,
    ivf_maps,
    sim_sky,
    sim_ivf,
    ra_wiener,
    ra_gradient,
    pair_table,
    sim_index,
    source_pixels,
    response,
):
    nsplit = pair_table.shape[0]
    rows, columns = sky_maps.shape
    fields = sim_index.shape[0] + 1
    assert columns & (columns - 1) == 0
    ivf = choose(sim_index, ivf_maps, sim_ivf)
    shape = (fields * PIECES, rows // PIECES, columns)
    slab_rows = -(-(fields + 1) // SLAB) * SLAB
    piece = pltpu.VMEM(shape, ivf.dtype)
    plane = pltpu.VMEM((rows, columns), jnp.float32)
    slabs = pltpu.VMEM((slab_rows, columns), jnp.float32)
    vmem = pl.BlockSpec(memory_space=pltpu.VMEM)
    away = pl.BlockSpec(memory_space=pl.ANY)
    pixels = pltpu.VMEM((1, source_pixels.shape[0]), jnp.int32)
    matrix = pltpu.VMEM(ra_wiener.shape, ra_wiener.dtype)
    return pl.pallas_call(
        functools.partial(estimator, nsplit),
        out_shape=jax.ShapeDtypeStruct((rows, columns), jnp.float32),
        in_specs=[pl.BlockSpec(memory_space=pltpu.SMEM)] * 2 + [vmem] + [away] * 4 + [vmem] * 2,
        out_specs=vmem,
        scratch_shapes=[pltpu.VMEM((sim_sky.shape[0] + 1, rows, columns), sky_maps.dtype), matrix, matrix, pixels, pixels]
        + [pltpu.SemaphoreType.DMA((4,))] + [piece] * 9
        + [pltpu.VMEM(shape, jnp.float32), plane, plane]
        + [pltpu.VMEM((fields, rows, columns), jnp.float32), plane, plane, plane]
        + [slabs] * 8
        + [pltpu.VMEM((rows * columns // LANES, LANES), jnp.float32)]
        + [pltpu.SemaphoreType.DMA((6, shape[0])), pltpu.SemaphoreType.DMA((6, shape[0]))]
        + [pltpu.SemaphoreType.DMA((4,)), pltpu.SemaphoreType.DMA((4,))],
        compiler_params=pltpu.CompilerParams(
            collective_id=0, has_side_effects=True, vmem_limit_bytes=56 << 20
        ),
    )(
        pair_table, sim_index, ivf.reshape(shape), sky_maps, sim_sky, ra_wiener, ra_gradient,
        source_pixels[None], response[None],
    )


def solution(mesh):
    in_specs = (
        P(("patch", "sim"), None),
        P(("patch", "sim"), None),
        P(None, ("patch", "sim"), None),
        P(None, ("patch", "sim"), None),
        P(),
        P(),
        P(),
        P(),
        P("patch"),
        P("patch"),
    )
    out_specs = P(("patch", "sim"), None)
    return jax.shard_map(
        on_device, mesh=mesh, in_specs=in_specs, out_specs=out_specs, check_vma=False
    )
```
